1024 devices in a mesh: chan: 32 (over x, y_lo, core), blk: 32 (over z, y_hi).
Axes of the slice: x: 8, y: 8 (y_hi: 4, y_lo: 2; y = y_hi * 2 + y_lo), z: 8, core: 2. Of those that a mesh axis runs over, the one named last changes fastest.
Arguments:
- t_matrix: bfloat16 [32, 4096, 1024], P('chan', 'blk'), may hold values from -0.1875 to 0.1875
- v_jacobi: bfloat16 [32, 1024, 1024], P('chan'), may hold values from -6 to 6
- channel_dims: int32 [32], P('chan'), may hold values from 128 to 1024, as said below
- owner_map: int32 [32], replicated, may hold values from 0 to 31, each once
Outputs:
- triplet_blocks: bfloat16 [32, 32, 4096, 128], P('chan', None, 'blk')
The draws below stay inside these ranges and needn't reach their ends.
Inputs may be any that keep to these rules, and one draw needn't show every extreme that they name: `channel_dims`: channel 0 has exactly 1024 live states; others vary.
All inputs are finite; a program needn't handle non-finite values.
Results may differ from the reference program's by a relative error of at most 0.0058.
Values may be sent and summed in bfloat16 or wider, within the bound.
A program may use at most 64 MiB of HBM per device.

```python
import jax
import jax.numpy as jnp
from jax import lax

NJ = 1024
CHANNELS = 32
NL = 4096
CB = 128
N_CHAN = 32


def draw_channel_dims(key, part):
    drawn = jax.random.randint(key, (CHANNELS,), NJ // 8, NJ + 1).astype(jnp.int32)
    return drawn.at[0].set(NJ)


def level_of(rng, extent, shards, low, top_value):
    def one(axis_at, shards_of):
        steps = jax.random.uniform(jax.random.fold_in(jax.random.fold_in(rng, 6), axis_at), (shards_of,), jnp.float32, low / len(shards), top_value / len(shards))
        return jnp.repeat(jnp.exp(steps), extent[axis_at] // shards_of).reshape((-1,) + (1,) * (len(extent) - axis_at - 1))

    level = one(*shards[0])
    for cut in shards[1:]:
        level = level * one(*cut)
    return level


def gaussian(stream_key, extent, width, bound, cuts=(), held_as=jnp.bfloat16):
    values = width * jax.random.normal(stream_key, extent, jnp.float32)
    if cuts:
        values = values * level_of(stream_key, extent, cuts, -0.22, 0.18)
    return jnp.clip(values, -bound, bound).astype(held_as)


def setup_inputs(seed: int = 0) -> dict:
    key_list = jax.random.split(jax.random.key(seed), 5)
    t_matrix = gaussian(key_list[0], (CHANNELS, NL, NJ), NJ ** -0.5, 0.1875, ((0, 32), (1, 32)))
    v_jacobi = gaussian(key_list[1], (CHANNELS, NJ, NJ), 1.0, 6.0, ((0, 32),))
    channel_dims = draw_channel_dims(jax.random.fold_in(key_list[4], 71), 0)
    owner_map = jax.random.permutation(key_list[3], N_CHAN).astype(jnp.int32)
    return {"t_matrix": t_matrix, "v_jacobi": v_jacobi, "channel_dims": channel_dims, "owner_map": owner_map}


def one_channel(packed):
    t_rows, v_raw, live = packed
    positions = jnp.arange(NJ, dtype=jnp.int32)
    kept_mask = (positions < live).astype(jnp.float32)
    v_float = v_raw.astype(jnp.float32)
    v_masked = ((v_float + v_float.T) * 0.5 * kept_mask[:, None] * kept_mask[None, :]).astype(jnp.bfloat16)
    weighted = jnp.dot(t_rows, v_masked, preferred_element_type=jnp.float32).astype(jnp.bfloat16)
    return jnp.dot(weighted, t_rows.T, preferred_element_type=jnp.float32).astype(jnp.bfloat16)


def reference(t_matrix, v_jacobi, channel_dims, owner_map):
    lab_rows = lax.map(one_channel, (t_matrix, v_jacobi, channel_dims))
    owners = jnp.arange(N_CHAN, dtype=jnp.int32)
    source_block = jnp.sum(owners[None, :] * (owner_map[None, :] == owners[:, None]).astype(jnp.int32), axis=1).astype(jnp.int32)
    col_blocks = lab_rows.reshape(CHANNELS, NL, N_CHAN, CB)
    picked = jnp.take(col_blocks, source_block, axis=2)
    return jnp.transpose(picked, (2, 0, 1, 3))
```

```python
import jax
import jax.numpy as jnp
from jax import lax
from jax.experimental import pallas as pl
from jax.experimental.pallas import tpu as pltpu
from jax.sharding import PartitionSpec as P

MESH = pl.DeviceIdType.MESH
NZ, NY = 8, 4
NX, NL, NC = 8, 2, 2
NCHAN = NX * NL * NC
ROWS, JAC, CB = 128, 1024, 128
PIECES = 4
PROWS = ROWS // PIECES
CHUNKS = 4
CROWS = ROWS // CHUNKS
Z_SHIFTS = (6, 7, 1, 2)
Y_SHIFTS = (1, 2, 3)
FAR = (3, 4, 5)
OWN = len(Z_SHIFTS)


def kernel(
    t_ref,
    v_ref,
    dims_ref,
    owner_ref,
    out_ref,
    tz,
    ty,
    v_raw,
    v_sym,
    wts,
    z_out,
    y_out,
    *rest,
):
    got = rest[:CHUNKS]
    stage = rest[CHUNKS : 2 * CHUNKS]
    (
        slots,
        local_sem,
        zs_sem,
        zr_sem,
        ys_sem,
        yr_sem,
        xs_sem,
        xr_sem,
        os_sem,
        or_sem,
    ) = rest[2 * CHUNKS :]

    chan = lax.axis_index("chan")
    blk = lax.axis_index("blk")
    z, y = blk // NY, blk % NY
    x, lo, core = chan // (NL * NC), (chan // NC) % NL, chan % NC

    def z_peer(shift):
        return (chan, ((z + shift) % NZ) * NY + y)

    def y_peer(shift):
        return (chan, z * NY + (y + shift) % NY)

    def owner_at(i):
        k, b = i % NX, 3 - i // NX
        dx = NX // 2 + (1 - 2 * (k % 2)) * ((k + 1) // 2)
        return (((x + dx) % NX) * NL + (lo + b // 2) % NL) * NC + (core + b % 2) % NC

    load_t = pltpu.make_async_copy(t_ref.at[0], tz.at[0], local_sem.at[0])
    load_v = pltpu.make_async_copy(v_ref.at[0], v_raw, local_sem.at[1])
    load_t.start()
    load_v.start()

    barrier = pltpu.get_barrier_semaphore()
    for shift in Z_SHIFTS:
        pl.semaphore_signal(barrier, 1, device_id=z_peer(shift), device_id_type=MESH)
    for shift in Y_SHIFTS:
        pl.semaphore_signal(barrier, 1, device_id=y_peer(shift), device_id_type=MESH)

    def greet(i, carry):
        pl.semaphore_signal(
            barrier, 1, device_id=(owner_at(i), blk), device_id_type=MESH
        )
        return carry

    lax.fori_loop(0, NCHAN - 1, greet, 0)

    places = [
        ((z - q // NY + NZ) % NZ) * NY + (y - q % NY + NY) % NY for q in range(NCHAN)
    ]

    def locate(d, carry):
        place = jnp.int32(0)
        for q in range(NCHAN):
            place = jnp.where(owner_ref[q] == d, places[q], place)
        slots[d] = place
        return carry

    lax.fori_loop(0, NCHAN, locate, 0)

    pl.semaphore_wait(barrier, len(Z_SHIFTS) + len(Y_SHIFTS) + NCHAN - 1)

    def piece(c):
        return pl.ds(c * PROWS, PROWS)

    def half(direction):
        return range(PIECES // 2) if direction == 0 else range(PIECES // 2, PIECES)

    def ring(buf, direction, hop, c, length, peer, s_sem, r_sem):
        sign = -1 if direction == 0 else 1
        src = t_ref.at[0] if hop == 1 else buf.at[(sign * (hop - 1)) % length]
        return pltpu.make_async_remote_copy(
            src_ref=src.at[piece(c)],
            dst_ref=buf.at[(sign * hop) % length, piece(c)],
            send_sem=s_sem.at[direction, hop - 1, c],
            recv_sem=r_sem.at[direction, hop - 1, c],
            device_id=peer(1 if direction == 0 else -1 + length),
            device_id_type=MESH,
        )

    z_last, y_last = NZ // 2, NY // 2
    z_copies = {
        (d, h, c): ring(tz, d, h, c, NZ, z_peer, zs_sem, zr_sem)
        for h in range(1, z_last + 1)
        for d in range(2)
        for c in (range(PIECES) if h < z_last else half(d))
    }
    y_copies = {
        (d, h, c): ring(ty, d, h, c, NY, y_peer, ys_sem, yr_sem)
        for h in range(1, y_last + 1)
        for d in range(2)
        for c in (range(PIECES) if h < y_last else half(d))
    }

    for c in range(PIECES):
        for d in range(2):
            z_copies[d, 1, c].start()
            y_copies[d, 1, c].start()

    def pass_on(copies, hop, c):
        for d in range(2):
            if (d, hop, c) in copies:
                copies[d, hop, c].wait_recv()
                if (d, hop + 1, c) in copies:
                    copies[d, hop + 1, c].start()

    load_v.wait()
    live = dims_ref[0]
    tile = 256
    for i in range(0, JAC, tile):
        row_ok = lax.broadcasted_iota(jnp.int32, (tile, tile), 0) + i < live
        for j in range(0, JAC, tile):
            col_ok = lax.broadcasted_iota(jnp.int32, (tile, tile), 1) + j < live
            a = v_raw[i : i + tile, j : j + tile].astype(jnp.float32)
            b = v_raw[j : j + tile, i : i + tile].astype(jnp.float32).T
            mean = jnp.where(row_ok & col_ok, (a + b) * 0.5, 0.0)
            v_sym[i : i + tile, j : j + tile] = mean.astype(jnp.bfloat16)

    def weigh(place, rows):
        for n in range(0, JAC, 256):
            wts[place * ROWS : (place + 1) * ROWS, n : n + 256] = jnp.dot(
                rows, v_sym[:, n : n + 256], preferred_element_type=jnp.float32
            ).astype(jnp.bfloat16)

    def product(first, count, cols):
        return lax.dot_general(
            wts[first * ROWS : (first + count) * ROWS, :],
            cols,
            (((1,), (1,)), ((), ())),
            preferred_element_type=jnp.float32,
        ).astype(jnp.bfloat16)

    def keep(block, dz, dy):
        for j in range(CHUNKS):
            got[j][dz, dy] = block[j * CROWS : (j + 1) * CROWS]

    def near(dz):
        keep(product(OWN, 1, tz[dz]), -dz % NZ, 0)

    def line(dy):
        made = product(0, OWN + 1, ty[dy])
        for s in range(OWN):
            for j in range(CHUNKS):
                at = s * ROWS + j * CROWS
                z_out[s, j, -dy % NY - 1] = made[at : at + CROWS]
        keep(made[OWN * ROWS :], 0, -dy % NY)

    def far(dz):
        made = product(OWN, 1 + len(Y_SHIFTS), tz[dz])
        keep(made[:ROWS], -dz % NZ, 0)
        for s in range(len(Y_SHIFTS)):
            for j in range(CHUNKS):
                at = (s + 1) * ROWS + j * CROWS
                y_out[s, j, FAR.index(-dz % NZ)] = made[at : at + CROWS]

    pass_on(z_copies, 1, 0)
    pass_on(z_copies, 1, 1)
    pass_on(y_copies, 1, 0)
    load_t.wait()
    weigh(OWN, tz[0])
    pass_on(z_copies, 1, 2)
    pass_on(z_copies, 1, 3)
    pass_on(y_copies, 1, 1)
    near(0)
    weigh(Z_SHIFTS.index(1), tz[1])
    pass_on(z_copies, 2, 0)
    weigh(Z_SHIFTS.index(7), tz[7])
    pass_on(z_copies, 2, 1)
    pass_on(y_copies, 1, 2)
    near(1)
    near(7)
    pass_on(z_copies, 2, 2)
    pass_on(z_copies, 2, 3)
    pass_on(y_copies, 1, 3)
    weigh(Z_SHIFTS.index(2), tz[2])
    pass_on(z_copies, 3, 0)
    weigh(Z_SHIFTS.index(6), tz[6])
    pass_on(z_copies, 3, 1)
    weigh(OWN + 1, ty[1])
    weigh(OWN + 3, ty[3])
    pass_on(z_copies, 3, 2)
    near(2)
    near(6)
    line(1)
    pass_on(z_copies, 3, 3)
    line(3)
    for c in range(PIECES):
        pass_on(y_copies, 2, c)
    line(2)

    z_sends = [
        [
            pltpu.make_async_remote_copy(
                src_ref=z_out.at[s, j],
                dst_ref=got[j].at[shift, pl.ds(1, NY - 1)],
                send_sem=xs_sem.at[j, s],
                recv_sem=xr_sem.at[j, s],
                device_id=z_peer(shift),
                device_id_type=MESH,
            )
            for s, shift in enumerate(Z_SHIFTS)
        ]
        for j in range(CHUNKS)
    ]
    y_sends = [
        [
            pltpu.make_async_remote_copy(
                src_ref=y_out.at[s, j],
                dst_ref=got[j].at[pl.ds(FAR[0], len(FAR)), shift],
                send_sem=xs_sem.at[j, OWN + s],
                recv_sem=xr_sem.at[j, OWN + s],
                device_id=y_peer(shift),
                device_id_type=MESH,
            )
            for s, shift in enumerate(Y_SHIFTS)
        ]
        for j in range(CHUNKS)
    ]
    for j in range(CHUNKS):
        for copy in z_sends[j]:
            copy.start()
    weigh(OWN + 2, ty[2])
    far(3)
    far(5)
    for c in range(PIECES):
        pass_on(z_copies, 4, c)
    far(4)
    for j in range(CHUNKS):
        for copy in y_sends[j]:
            copy.start()

    def to_owner(j, i):
        return pltpu.make_async_remote_copy(
            src_ref=stage[j].at[i],
            dst_ref=out_ref.at[0, chan, pl.ds(j * CROWS, CROWS)],
            send_sem=os_sem.at[j],
            recv_sem=or_sem.at[0],
            device_id=(owner_at(i), blk),
            device_id_type=MESH,
        )

    for j in range(CHUNKS):
        for copy in z_sends[j] + y_sends[j]:
            copy.wait_recv()

        def pick(i, carry):
            place = slots[owner_at(i)]
            stage[j][i] = got[j][place // NY, place % NY]
            return carry

        lax.fori_loop(0, NCHAN, pick, 0)

        def send(i, carry):
            to_owner(j, i).start()
            return carry

        lax.fori_loop(0, NCHAN - 1, send, 0)
        pltpu.make_async_copy(
            stage[j].at[NCHAN - 1],
            out_ref.at[0, chan, pl.ds(j * CROWS, CROWS)],
            or_sem.at[0],
        ).start()

    for copies in (z_copies, y_copies):
        for copy in copies.values():
            copy.wait_send()
    for j in range(CHUNKS):
        for copy in z_sends[j] + y_sends[j]:
            copy.wait_send()
        sent = stage[j].at[pl.ds(0, NCHAN - 1)]
        pltpu.make_async_copy(sent, sent, os_sem.at[j]).wait()
    pltpu.make_async_copy(out_ref, out_ref, or_sem.at[0]).wait()


def per_device(t_matrix, v_jacobi, channel_dims, owner_map):
    bf16 = jnp.bfloat16
    any_spec = pl.BlockSpec(memory_space=pl.ANY)
    smem_spec = pl.BlockSpec(memory_space=pltpu.SMEM)
    return pl.pallas_call(
        kernel,
        out_shape=jax.ShapeDtypeStruct((1, NCHAN, ROWS, CB), bf16),
        in_specs=[any_spec, any_spec, smem_spec, smem_spec],
        out_specs=any_spec,
        scratch_shapes=[
            pltpu.VMEM((NZ, ROWS, JAC), bf16),
            pltpu.VMEM((NY, ROWS, JAC), bf16),
            pltpu.VMEM((JAC, JAC), bf16),
            pltpu.VMEM((JAC, JAC), bf16),
            pltpu.VMEM(((OWN + 1 + len(Y_SHIFTS)) * ROWS, JAC), bf16),
            pltpu.VMEM((OWN, CHUNKS, NY - 1, CROWS, CB), bf16),
            pltpu.VMEM((len(Y_SHIFTS), CHUNKS, len(FAR), CROWS, CB), bf16),
        ]
        + [pltpu.VMEM((NZ, NY, CROWS, CB), bf16)] * CHUNKS
        + [pltpu.VMEM((NCHAN, CROWS, CB), bf16)] * CHUNKS
        + [
            pltpu.SMEM((NCHAN,), jnp.int32),
            pltpu.SemaphoreType.DMA((2,)),
            pltpu.SemaphoreType.DMA((2, NZ // 2, PIECES)),
            pltpu.SemaphoreType.DMA((2, NZ // 2, PIECES)),
            pltpu.SemaphoreType.DMA((2, NY // 2, PIECES)),
            pltpu.SemaphoreType.DMA((2, NY // 2, PIECES)),
            pltpu.SemaphoreType.DMA((CHUNKS, OWN + len(Y_SHIFTS))),
            pltpu.SemaphoreType.DMA((CHUNKS, OWN + len(Y_SHIFTS))),
            pltpu.SemaphoreType.DMA((CHUNKS,)),
            pltpu.SemaphoreType.DMA((1,)),
        ],
        compiler_params=pltpu.CompilerParams(collective_id=0, has_side_effects=True),
        name="lab_blocks",
    )(t_matrix, v_jacobi, channel_dims, owner_map)


def solution(mesh):
    in_specs = (P("chan", "blk", None), P("chan", None, None), P("chan"), P())
    out_specs = P("chan", None, "blk", None)
    return jax.shard_map(
        per_device, mesh=mesh, in_specs=in_specs, out_specs=out_specs, check_vma=False
    )
```

```python
import jax
import jax.numpy as jnp
from jax import lax
from jax.experimental import pallas as pl
from jax.experimental.pallas import tpu as pltpu
from jax.sharding import PartitionSpec as P

MESH = pl.DeviceIdType.MESH
NZ, NY = 8, 4
NX, NL, NC = 8, 2, 2
NCHAN = NX * NL * NC
ROWS, JAC, CB = 128, 1024, 128
PIECES = 4
PROWS = ROWS // PIECES
CHUNKS = 4
CROWS = ROWS // CHUNKS
Z_SHIFTS = (6, 7, 1, 2)
Y_SHIFTS = (1, 2, 3)
FAR = (3, 4, 5)
OWN = len(Z_SHIFTS)


def kernel(
    t_ref,
    v_ref,
    dims_ref,
    owner_ref,
    out_ref,
    tz,
    ty,
    v_raw,
    v_sym,
    wts,
    z_out,
    y_out,
    *rest,
):
    got = rest[:CHUNKS]
    stage = rest[CHUNKS : 2 * CHUNKS]
    (
        slots,
        local_sem,
        zs_sem,
        zr_sem,
        ys_sem,
        yr_sem,
        xs_sem,
        xr_sem,
        os_sem,
        or_sem,
    ) = rest[2 * CHUNKS :]

    chan = lax.axis_index("chan")
    blk = lax.axis_index("blk")
    z, y = blk // NY, blk % NY
    x, lo, core = chan // (NL * NC), (chan // NC) % NL, chan % NC

    def z_peer(shift):
        return (chan, ((z + shift) % NZ) * NY + y)

    def y_peer(shift):
        return (chan, z * NY + (y + shift) % NY)

    def owner_at(i):
        k, b = i // (NL * NC), NL * NC - 1 - i % (NL * NC)
        dx = NX // 2 + (1 - 2 * (k % 2)) * ((k + 1) // 2)
        return (((x + dx) % NX) * NL + (lo + b // 2) % NL) * NC + (core + b % 2) % NC

    load_t = pltpu.make_async_copy(t_ref.at[0], tz.at[0], local_sem.at[0])
    load_v = pltpu.make_async_copy(v_ref.at[0], v_raw, local_sem.at[1])
    load_t.start()
    load_v.start()

    barrier = pltpu.get_barrier_semaphore()
    for shift in Z_SHIFTS:
        pl.semaphore_signal(barrier, 1, device_id=z_peer(shift), device_id_type=MESH)
    for shift in Y_SHIFTS:
        pl.semaphore_signal(barrier, 1, device_id=y_peer(shift), device_id_type=MESH)

    def greet(i, carry):
        pl.semaphore_signal(
            barrier, 1, device_id=(owner_at(i), blk), device_id_type=MESH
        )
        return carry

    lax.fori_loop(0, NCHAN - 1, greet, 0)

    places = [
        ((z - q // NY + NZ) % NZ) * NY + (y - q % NY + NY) % NY for q in range(NCHAN)
    ]

    def locate(d, carry):
        place = jnp.int32(0)
        for q in range(NCHAN):
            place = jnp.where(owner_ref[q] == d, places[q], place)
        slots[d] = place
        return carry

    lax.fori_loop(0, NCHAN, locate, 0)

    pl.semaphore_wait(barrier, len(Z_SHIFTS) + len(Y_SHIFTS) + NCHAN - 1)

    def piece(c):
        return pl.ds(c * PROWS, PROWS)

    def half(direction):
        return range(PIECES // 2) if direction == 0 else range(PIECES // 2, PIECES)

    def ring(buf, direction, hop, c, length, peer, s_sem, r_sem):
        sign = -1 if direction == 0 else 1
        src = t_ref.at[0] if hop == 1 else buf.at[(sign * (hop - 1)) % length]
        return pltpu.make_async_remote_copy(
            src_ref=src.at[piece(c)],
            dst_ref=buf.at[(sign * hop) % length, piece(c)],
            send_sem=s_sem.at[direction, hop - 1, c],
            recv_sem=r_sem.at[direction, hop - 1, c],
            device_id=peer(1 if direction == 0 else -1 + length),
            device_id_type=MESH,
        )

    z_last, y_last = NZ // 2, NY // 2
    z_copies = {
        (d, h, c): ring(tz, d, h, c, NZ, z_peer, zs_sem, zr_sem)
        for h in range(1, z_last + 1)
        for d in range(2)
        for c in (range(PIECES) if h < z_last else half(d))
    }
    y_copies = {
        (d, h, c): ring(ty, d, h, c, NY, y_peer, ys_sem, yr_sem)
        for h in range(1, y_last + 1)
        for d in range(2)
        for c in (range(PIECES) if h < y_last else half(d))
    }

    for c in range(PIECES):
        for d in range(2):
            z_copies[d, 1, c].start()
            y_copies[d, 1, c].start()

    def pass_on(copies, hop, c):
        for d in range(2):
            if (d, hop, c) in copies:
                copies[d, hop, c].wait_recv()
                if (d, hop + 1, c) in copies:
                    copies[d, hop + 1, c].start()

    load_v.wait()
    live = dims_ref[0]
    tile = 256
    for i in range(0, JAC, tile):
        row_ok = lax.broadcasted_iota(jnp.int32, (tile, tile), 0) + i < live
        for j in range(0, JAC, tile):
            col_ok = lax.broadcasted_iota(jnp.int32, (tile, tile), 1) + j < live
            a = v_raw[i : i + tile, j : j + tile].astype(jnp.float32)
            b = v_raw[j : j + tile, i : i + tile].astype(jnp.float32).T
            mean = jnp.where(row_ok & col_ok, (a + b) * 0.5, 0.0)
            v_sym[i : i + tile, j : j + tile] = mean.astype(jnp.bfloat16)

    def weigh(place, rows):
        for n in range(0, JAC, 256):
            wts[place * ROWS : (place + 1) * ROWS, n : n + 256] = jnp.dot(
                rows, v_sym[:, n : n + 256], preferred_element_type=jnp.float32
            ).astype(jnp.bfloat16)

    def product(first, count, cols):
        return lax.dot_general(
            wts[first * ROWS : (first + count) * ROWS, :],
            cols,
            (((1,), (1,)), ((), ())),
            preferred_element_type=jnp.float32,
        ).astype(jnp.bfloat16)

    def keep(block, dz, dy):
        for j in range(CHUNKS):
            got[j][dz, dy] = block[j * CROWS : (j + 1) * CROWS]

    def near(dz):
        keep(product(OWN, 1, tz[dz]), -dz % NZ, 0)

    def line(dy):
        made = product(0, OWN + 1, ty[dy])
        for s in range(OWN):
            for j in range(CHUNKS):
                at = s * ROWS + j * CROWS
                z_out[s, j, -dy % NY - 1] = made[at : at + CROWS]
        keep(made[OWN * ROWS :], 0, -dy % NY)

    def far(dz):
        made = product(OWN, 1 + len(Y_SHIFTS), tz[dz])
        keep(made[:ROWS], -dz % NZ, 0)
        for s in range(len(Y_SHIFTS)):
            for j in range(CHUNKS):
                at = (s + 1) * ROWS + j * CROWS
                y_out[s, j, FAR.index(-dz % NZ)] = made[at : at + CROWS]

    pass_on(z_copies, 1, 0)
    pass_on(z_copies, 1, 1)
    pass_on(y_copies, 1, 0)
    load_t.wait()
    weigh(OWN, tz[0])
    pass_on(z_copies, 1, 2)
    pass_on(z_copies, 1, 3)
    pass_on(y_copies, 1, 1)
    near(0)
    weigh(Z_SHIFTS.index(1), tz[1])
    pass_on(z_copies, 2, 0)
    weigh(Z_SHIFTS.index(7), tz[7])
    pass_on(z_copies, 2, 1)
    pass_on(y_copies, 1, 2)
    near(1)
    near(7)
    pass_on(z_copies, 2, 2)
    pass_on(z_copies, 2, 3)
    pass_on(y_copies, 1, 3)
    weigh(Z_SHIFTS.index(2), tz[2])
    pass_on(z_copies, 3, 0)
    weigh(Z_SHIFTS.index(6), tz[6])
    pass_on(z_copies, 3, 1)
    weigh(OWN + 1, ty[1])
    weigh(OWN + 3, ty[3])
    pass_on(z_copies, 3, 2)
    near(2)
    near(6)
    line(1)
    pass_on(z_copies, 3, 3)
    line(3)
    for c in range(PIECES):
        pass_on(y_copies, 2, c)
    line(2)

    z_sends = [
        [
            pltpu.make_async_remote_copy(
                src_ref=z_out.at[s, j],
                dst_ref=got[j].at[shift, pl.ds(1, NY - 1)],
                send_sem=xs_sem.at[j, s],
                recv_sem=xr_sem.at[j, s],
                device_id=z_peer(shift),
                device_id_type=MESH,
            )
            for s, shift in enumerate(Z_SHIFTS)
        ]
        for j in range(CHUNKS)
    ]
    y_sends = [
        [
            pltpu.make_async_remote_copy(
                src_ref=y_out.at[s, j],
                dst_ref=got[j].at[pl.ds(FAR[0], len(FAR)), shift],
                send_sem=xs_sem.at[j, OWN + s],
                recv_sem=xr_sem.at[j, OWN + s],
                device_id=y_peer(shift),
                device_id_type=MESH,
            )
            for s, shift in enumerate(Y_SHIFTS)
        ]
        for j in range(CHUNKS)
    ]
    for j in range(CHUNKS):
        for copy in z_sends[j]:
            copy.start()
    weigh(OWN + 2, ty[2])
    far(3)
    far(5)
    for c in range(PIECES):
        pass_on(z_copies, 4, c)
    far(4)
    for j in range(CHUNKS):
        for copy in y_sends[j]:
            copy.start()

    def to_owner(j, i):
        return pltpu.make_async_remote_copy(
            src_ref=stage[j].at[i],
            dst_ref=out_ref.at[0, chan, pl.ds(j * CROWS, CROWS)],
            send_sem=os_sem.at[j],
            recv_sem=or_sem.at[0],
            device_id=(owner_at(i), blk),
            device_id_type=MESH,
        )

    for j in range(CHUNKS):
        for copy in z_sends[j] + y_sends[j]:
            copy.wait_recv()

        def pick(i, carry):
            place = slots[owner_at(i)]
            stage[j][i] = got[j][place // NY, place % NY]
            return carry

        lax.fori_loop(0, NCHAN, pick, 0)

        def send(i, carry):
            to_owner(j, i).start()
            return carry

        lax.fori_loop(0, NCHAN - 1, send, 0)
        pltpu.make_async_copy(
            stage[j].at[NCHAN - 1],
            out_ref.at[0, chan, pl.ds(j * CROWS, CROWS)],
            or_sem.at[0],
        ).start()

    for copies in (z_copies, y_copies):
        for copy in copies.values():
            copy.wait_send()
    for j in range(CHUNKS):
        for copy in z_sends[j] + y_sends[j]:
            copy.wait_send()
        sent = stage[j].at[pl.ds(0, NCHAN - 1)]
        pltpu.make_async_copy(sent, sent, os_sem.at[j]).wait()
    pltpu.make_async_copy(out_ref, out_ref, or_sem.at[0]).wait()


def per_device(t_matrix, v_jacobi, channel_dims, owner_map):
    bf16 = jnp.bfloat16
    any_spec = pl.BlockSpec(memory_space=pl.ANY)
    smem_spec = pl.BlockSpec(memory_space=pltpu.SMEM)
    return pl.pallas_call(
        kernel,
        out_shape=jax.ShapeDtypeStruct((1, NCHAN, ROWS, CB), bf16),
        in_specs=[any_spec, any_spec, smem_spec, smem_spec],
        out_specs=any_spec,
        scratch_shapes=[
            pltpu.VMEM((NZ, ROWS, JAC), bf16),
            pltpu.VMEM((NY, ROWS, JAC), bf16),
            pltpu.VMEM((JAC, JAC), bf16),
            pltpu.VMEM((JAC, JAC), bf16),
            pltpu.VMEM(((OWN + 1 + len(Y_SHIFTS)) * ROWS, JAC), bf16),
            pltpu.VMEM((OWN, CHUNKS, NY - 1, CROWS, CB), bf16),
            pltpu.VMEM((len(Y_SHIFTS), CHUNKS, len(FAR), CROWS, CB), bf16),
        ]
        + [pltpu.VMEM((NZ, NY, CROWS, CB), bf16)] * CHUNKS
        + [pltpu.VMEM((NCHAN, CROWS, CB), bf16)] * CHUNKS
        + [
            pltpu.SMEM((NCHAN,), jnp.int32),
            pltpu.SemaphoreType.DMA((2,)),
            pltpu.SemaphoreType.DMA((2, NZ // 2, PIECES)),
            pltpu.SemaphoreType.DMA((2, NZ // 2, PIECES)),
            pltpu.SemaphoreType.DMA((2, NY // 2, PIECES)),
            pltpu.SemaphoreType.DMA((2, NY // 2, PIECES)),
            pltpu.SemaphoreType.DMA((CHUNKS, OWN + len(Y_SHIFTS))),
            pltpu.SemaphoreType.DMA((CHUNKS, OWN + len(Y_SHIFTS))),
            pltpu.SemaphoreType.DMA((CHUNKS,)),
            pltpu.SemaphoreType.DMA((1,)),
        ],
        compiler_params=pltpu.CompilerParams(
            collective_id=0, has_side_effects=True, vmem_limit_bytes=52 * 2**20
        ),
        name="lab_blocks",
    )(t_matrix, v_jacobi, channel_dims, owner_map)


def solution(mesh):
    in_specs = (P("chan", "blk", None), P("chan", None, None), P("chan"), P())
    out_specs = P("chan", None, "blk", None)
    return jax.shard_map(
        per_device, mesh=mesh, in_specs=in_specs, out_specs=out_specs, check_vma=False
    )
```
